32 devices in a mesh: win: 8 (over y, x, core), seq: 4 (over z).
Axes of the slice: x: 2, y: 2, z: 4, core: 2. Of those that a mesh axis runs over, the one named last changes fastest.
Arguments:
- qkv_grid: bfloat16 [90, 8, 32, 4608], P(None, 'win', 'seq'), may hold values from -160 to 160
- tokens: bfloat16 [90, 8, 32, 1536], P(None, 'win', 'seq'), may hold values from -6 to 6
- out_weight: bfloat16 [1536, 1536], replicated, may hold values from -0.625 to 0.625
- regions: int32 [90, 8, 32], P(None, 'win'), may hold values from 0 to 2, as said below
Outputs:
- mixed: bfloat16 [90, 8, 32, 1536], P(None, 'win', 'seq')
The draws below stay inside these ranges and needn't reach their ends.
Inputs may be any that keep to these rules, and one draw needn't show every extreme that they name: `regions`: columns 2m and 2m+1 of a window always have the same region id.
All inputs are finite; a program needn't handle non-finite values.
Results may differ from the reference program's by a relative error of at most 0.01.
Values may be sent and summed in bfloat16 or wider, within the bound.
A program may use at most 128 MiB of HBM per device.

```python
import jax
import jax.numpy as jnp
from jax import lax

D = 1536
HEADS = 16
HD = 96
WH = 30
WW = 32
LATW = 3
REGIONS = 3
LAT = 90
LONWIN = 8


def draw_regions(key, part):
    region_pairs = jax.random.randint(jax.random.fold_in(key, 11), (LAT, LONWIN, WW // 2), 0, REGIONS)
    return jnp.repeat(region_pairs, 2, axis=2).astype(jnp.int32)


def draw_qkv_grid(key, part):
    columns = LONWIN * WW
    base = jax.random.normal(jax.random.fold_in(key, 21), (LAT, columns, 3, HEADS, HD), jnp.float32)
    base = jnp.clip(base, -6.0, 6.0)
    grid = jnp.roll(base, (WH // 2, WW // 2), (0, 1))
    return grid.reshape(LAT, LONWIN, WW, 3 * D).astype(jnp.bfloat16)


def block_scale(rng, extent, pieces, smallest, high):
    def one(dim, parts):
        heights = jax.random.uniform(jax.random.fold_in(jax.random.fold_in(rng, 6), dim), (parts,), jnp.float32, smallest / len(pieces), high / len(pieces))
        return jnp.repeat(jnp.exp(heights), extent[dim] // parts).reshape((-1,) + (1,) * (len(extent) - dim - 1))

    loudness = one(*pieces[0])
    for cut in pieces[1:]:
        loudness = loudness * one(*cut)
    return loudness


def normal_values(rng, dims, spread, most, cuts=(), dtype=jnp.bfloat16):
    drawn = jax.random.normal(rng, dims, jnp.float32) * spread
    if len(cuts) > 0:
        drawn = block_scale(rng, dims, cuts, -0.22, 0.18) * drawn
    return jnp.clip(drawn, min=-most, max=most).astype(dtype)


def setup_inputs(seed: int = 0) -> dict:
    key_list = jax.random.split(jax.random.key(seed), 5)
    qkv_grid = draw_qkv_grid(jax.random.fold_in(key_list[4], 71), 0)
    tokens = normal_values(key_list[1], (LAT, LONWIN, WW, D), 1.0, 6.0, ((1, 8), (2, 4)))
    out_weight = normal_values(key_list[2], (D, D), (D // 16) ** -0.5, 0.625)
    regions = draw_regions(jax.random.fold_in(key_list[4], 71), 0)
    return {"qkv_grid": qkv_grid, "tokens": tokens, "out_weight": out_weight, "regions": regions}


def attend(window_block, labels):
    queries = window_block[:, 0].astype(jnp.float32)
    key_rows = window_block[:, 1].astype(jnp.float32)
    values = window_block[:, 2].astype(jnp.float32)
    scores = jnp.einsum("qhd,khd->hqk", queries, key_rows) * (HD ** -0.5)
    allowed = labels[:, None] == labels[None, :]
    scores = jnp.where(allowed[None], scores, -1e30)
    largest = jnp.max(scores, axis=-1, keepdims=True)
    weights = jnp.exp(scores - largest)
    soft_weights = (weights / jnp.sum(weights, axis=-1, keepdims=True)).astype(jnp.bfloat16)
    result = jnp.einsum("hqk,khd->qhd", soft_weights.astype(jnp.float32), values)
    return result.astype(jnp.bfloat16)


def one_window(paired):
    return attend(paired[0], paired[1])


def reference(qkv_grid, tokens, out_weight, regions):
    columns = LONWIN * WW
    grid = qkv_grid.reshape(LAT, columns, 3, HEADS, HD)
    shifted = jnp.roll(grid, (-(WH // 2), -(WW // 2)), (0, 1))
    blocks = shifted.reshape(LATW, WH, LONWIN, WW, 3, HEADS, HD).transpose(0, 2, 1, 3, 4, 5, 6)
    blocks = blocks.reshape(LATW * LONWIN, WH * WW, 3, HEADS, HD)
    labels = regions.reshape(LATW, WH, LONWIN, WW).transpose(0, 2, 1, 3).reshape(LATW * LONWIN, WH * WW)
    attended = lax.map(one_window, (blocks, labels))
    attended = attended.reshape(LATW, LONWIN, WH, WW, D).transpose(0, 2, 1, 3, 4).reshape(LAT, columns, D)
    restored = jnp.roll(attended, (WH // 2, WW // 2), (0, 1))
    projected = jnp.dot(restored.reshape(LAT * columns, D), out_weight, preferred_element_type=jnp.float32)
    total = projected + tokens.reshape(LAT * columns, D).astype(jnp.float32)
    return total.astype(jnp.bfloat16).reshape(LAT, LONWIN, WW, D)
```

```python
import functools

import jax
import jax.numpy as jnp
from jax import lax
from jax.experimental import pallas as pl
from jax.experimental.pallas import tpu as pltpu
from jax.sharding import PartitionSpec as P

D = 1536
HEADS = 16
HD = 96
WH = 30
WW = 32


def from_behind(block, axis, distance):
    devices = range(lax.axis_size(axis))
    route = [((i - distance) % len(devices), i) for i in devices]
    return lax.ppermute(block, axis, route)


def attend(window_block, labels):
    queries = window_block[:, 0]
    key_rows = window_block[:, 1]
    values = window_block[:, 2]
    scores = jnp.einsum(
        "qhd,khd->hqk", queries, key_rows, preferred_element_type=jnp.float32
    ) * HD ** (-0.5)
    allowed = labels[:, None] == labels[None, :]
    scores = jnp.where(allowed[None], scores, -1e30)
    largest = jnp.max(scores, axis=-1, keepdims=True)
    weights = jnp.exp(scores - largest)
    soft_weights = (weights / jnp.sum(weights, axis=-1, keepdims=True)).astype(jnp.bfloat16)
    result = jnp.einsum("hqk,khd->qhd", soft_weights, values, preferred_element_type=jnp.float32)
    return result.astype(jnp.bfloat16)


def one_window(paired):
    return attend(paired[0], paired[1])


def window_attention(flat_grid, labels_flat):
    row_total, col_total, three, heads_here, head_size = flat_grid.shape
    bands = row_total // WH
    window_count = col_total // WW
    blocks = flat_grid.reshape(bands, WH, window_count, WW, three, heads_here, head_size)
    blocks = blocks.transpose(0, 2, 1, 3, 4, 5, 6).reshape(
        bands * window_count, WH * WW, three, heads_here, head_size
    )
    labels = (
        labels_flat.reshape(bands, WH, window_count, WW)
        .transpose(0, 2, 1, 3)
        .reshape(bands * window_count, WH * WW)
    )
    attended = lax.map(one_window, (blocks, labels))
    attended = attended.reshape(bands, window_count, WH, WW, heads_here, head_size).transpose(
        0, 2, 1, 3, 4, 5
    )
    return attended.reshape(row_total, col_total, heads_here, head_size)


def general_device(qkv_grid, tokens, out_weight, regions):
    seq_count = lax.axis_size("seq")
    lat_rows, win_count, col_count, packed_width = qkv_grid.shape
    labels_local = regions.reshape(lat_rows, win_count * WW)
    half_cols = WW // 2
    half_rows = WH // 2
    group_heads = HEADS // seq_count
    split_heads = qkv_grid.reshape(lat_rows, win_count, col_count, 3, seq_count, group_heads, HD)
    gathered = lax.all_to_all(split_heads, "seq", split_axis=4, concat_axis=2, tiled=True)
    flat_grid = gathered.reshape(lat_rows, win_count * WW, 3, group_heads, HD)
    arriving = from_behind(flat_grid[:, :half_cols], "win", -1)
    shifted = jnp.concatenate([flat_grid[:, half_cols:], arriving], axis=1)
    shifted = jnp.roll(shifted, -half_rows, axis=0)
    result = window_attention(shifted, labels_local)
    result = jnp.roll(result, half_rows, axis=0)
    leaving = from_behind(result[:, -half_cols:], "win", 1)
    result = jnp.concatenate([leaving, result[:, :-half_cols]], axis=1)
    attended = result.reshape(lat_rows, win_count, WW, 1, group_heads, HD)
    returned = lax.all_to_all(attended, "seq", split_axis=2, concat_axis=3, tiled=True)
    mixed_in = returned.reshape(lat_rows, win_count, col_count, D)
    projected = jnp.dot(mixed_in.reshape(-1, D), out_weight, preferred_element_type=jnp.float32)
    total = projected + tokens.reshape(-1, D).astype(jnp.float32)
    return total.astype(jnp.bfloat16).reshape(tokens.shape)


LANES = 128
ROWS8 = 8
FAR = -1e30
LOG2E = 1.4426950408889634
REGION_SLOTS = 3


def head_span(head):
    first = head * HD // LANES
    last = ((head + 1) * HD - 1) // LANES
    return first, last + 1, head * HD - first * LANES


def spare_lane(head):
    first, last, start = head_span(head)
    return 0 if start > 0 else HD


def fused_kernel(
    windows,
    members,
    bands,
    cols,
    qkv_ref,
    tokens_ref,
    weight_ref,
    label_ref,
    out_ref,
    arrived,
    label_v,
    weight_v,
    token_v,
    q_h,
    k_h,
    v_h,
    result,
    gathered,
    out_v,
    send_sem,
    recv_sem,
    own_sem,
    back_send,
    back_recv,
    back_own,
    token_sem,
    out_sem,
    misc_sem,
):
    half_rows = WH // 2
    half_n = members // 2
    group = D // members
    heads = HEADS // members
    block = WH * cols
    lat = bands * WH
    w = lax.axis_index("win")
    s = lax.axis_index("seq")
    low = 1 - s // half_n
    home = lax.rem(w + windows - low, windows)
    me = lax.rem(s + half_n, members)

    def member_at(distance):
        return lax.rem(me + distance, members)

    def device_of(member):
        seat = lax.rem(member + half_n, members)
        column = lax.rem(home + 1 - seat // half_n, windows)
        return {"win": column, "seq": seat}

    def grid_row(band, part):
        return lax.rem(half_rows * (2 * band + part + 1), lat)

    def features(kind, member):
        return pl.ds(pl.multiple_of(kind * D + member * group, LANES), group)

    def outgoing(band, distance, kind, part):
        target = member_at(distance)
        return pltpu.make_async_remote_copy(
            src_ref=qkv_ref.at[pl.ds(grid_row(band, part), half_rows), :, features(kind, target)],
            dst_ref=arrived.at[band, kind, me, pl.ds(part * half_rows, half_rows)],
            send_sem=send_sem.at[band, distance - 1, kind, part],
            recv_sem=recv_sem.at[band, distance - 1, kind, part],
            device_id=device_of(target),
            device_id_type=pl.DeviceIdType.MESH,
        )

    def own(band, kind, part):
        return pltpu.make_async_copy(
            qkv_ref.at[pl.ds(grid_row(band, part), half_rows), :, features(kind, me)],
            arrived.at[band, kind, me, pl.ds(part * half_rows, half_rows)],
            own_sem.at[band, kind, part],
        )

    def token_copy(band, part):
        return pltpu.make_async_copy(
            tokens_ref.at[pl.ds(grid_row(band, part), half_rows)],
            token_v.at[band, pl.ds(part * half_rows, half_rows)],
            token_sem.at[band, part],
        )

    def out_copy(band, part):
        return pltpu.make_async_copy(
            out_v.at[band, pl.ds(part * half_rows, half_rows)],
            out_ref.at[pl.ds(grid_row(band, part), half_rows)],
            out_sem.at[band, part],
        )

    def rows_of(member):
        return pl.ds(pl.multiple_of(member * block, block), block)

    def homeward(band, distance):
        target = member_at(distance)
        return pltpu.make_async_remote_copy(
            src_ref=result.at[band, rows_of(target)],
            dst_ref=gathered.at[band, :, features(0, me)],
            send_sem=back_send.at[band, distance - 1],
            recv_sem=back_recv.at[band, distance - 1],
            device_id=device_of(target),
            device_id_type=pl.DeviceIdType.MESH,
        )

    def stay(band):
        return pltpu.make_async_copy(
            result.at[band, rows_of(me)],
            gathered.at[band, :, features(0, me)],
            back_own.at[band],
        )

    label_copy = pltpu.make_async_copy(label_ref, label_v, misc_sem.at[0])
    weight_copy = pltpu.make_async_copy(weight_ref, weight_v, misc_sem.at[1])

    barrier = pltpu.get_barrier_semaphore()
    for distance in range(1, members):
        pl.semaphore_signal(
            barrier,
            inc=1,
            device_id=device_of(member_at(distance)),
            device_id_type=pl.DeviceIdType.MESH,
        )
    pl.semaphore_wait(barrier, members - 1)

    pieces = [(kind, part) for kind in range(3) for part in range(2)]

    def launch(band, carry):
        for kind, part in pieces:
            for distance in range(1, members):
                outgoing(band, distance, kind, part).start()
        for kind, part in pieces:
            own(band, kind, part).start()
        return carry

    lax.fori_loop(0, bands, launch, 0)
    label_copy.start()
    weight_copy.start()
    for band in range(bands):
        for part in range(2):
            token_copy(band, part).start()
    label_copy.wait()

    lane = lax.broadcasted_iota(jnp.int32, (block, LANES), 1)
    slot = lax.rem(lane, 32).astype(jnp.float32)

    def prepare(band, member):
        rows = rows_of(member)
        label = label_v[band, rows, :].astype(jnp.float32)
        same = slot == label
        query_fill = jnp.where(same, FAR, 0.0)
        key_fill = jnp.where(same, 0.0, jnp.where(slot < REGION_SLOTS, 1.0, 0.0))
        ones = jnp.ones((block, LANES), jnp.float32)
        for kind, target, fill in ((0, q_h, query_fill), (1, k_h, key_fill), (2, v_h, ones)):
            wide = arrived[band, kind, member].astype(jnp.float32).reshape(block, group)
            for head in range(heads):
                first, last, start = head_span(head)
                for tile in range(first, last):
                    place = lane + (tile - first) * LANES
                    inside = (place >= start) & (place < start + HD)
                    chosen = jnp.where(inside, wide[:, tile * LANES : (tile + 1) * LANES], fill)
                    spot = (tile - first) * LANES
                    target[head, rows, spot : spot + LANES] = chosen.astype(jnp.bfloat16)

    def attend_band(band, carry):
        for kind, part in pieces:
            own(band, kind, part).wait()
            for distance in range(1, members):
                outgoing(band, distance, kind, part).wait_recv()

        def prepare_step(member, inner):
            prepare(band, member)
            return inner

        lax.fori_loop(0, members, prepare_step, 0)

        def query_step(step, inner):
            target = member_at(step + 1)
            rows = rows_of(target)
            tiles = [None] * (group // LANES)
            for head in range(heads):
                first, last, start = head_span(head)
                width = (last - first) * LANES
                scores = lax.dot_general(
                    q_h[head, rows, :width],
                    k_h[head, :, :width],
                    (((1,), (1,)), ((), ())),
                    preferred_element_type=jnp.float32,
                )
                largest = jnp.max(scores, axis=-1, keepdims=True)
                weights = jnp.exp2((scores - largest) * (HD ** (-0.5) * LOG2E))
                mixed = jnp.dot(
                    weights.astype(jnp.bfloat16),
                    v_h[head, :, :width],
                    preferred_element_type=jnp.float32,
                )
                spare = spare_lane(head)
                mixed = mixed * (1.0 / mixed[:, spare : spare + 1])
                for tile in range(first, last):
                    piece = mixed[:, (tile - first) * LANES : (tile - first + 1) * LANES]
                    if tiles[tile] is None:
                        tiles[tile] = piece
                    else:
                        tiles[tile] = jnp.where(lane < head * HD - tile * LANES, tiles[tile], piece)
            for tile, value in enumerate(tiles):
                result[band, rows, tile * LANES : (tile + 1) * LANES] = value.astype(jnp.bfloat16)

            @pl.when(step < members - 1)
            def _():
                homeward(band, step + 1).start()

            @pl.when(step == members - 1)
            def _():
                stay(band).start()

            return inner

        lax.fori_loop(0, members, query_step, 0)
        return carry

    lax.fori_loop(0, bands, attend_band, 0)

    weight_copy.wait()

    def project(band, carry):
        stay(band).wait()
        for part in range(2):
            token_copy(band, part).wait()
        for distance in range(1, members):
            homeward(band, distance).wait_recv()
        for start in range(0, D, group):
            columns = slice(start, start + group)
            total = jnp.dot(
                gathered[band], weight_v[:, columns], preferred_element_type=jnp.float32
            )
            total = total.reshape(WH, cols, group) + token_v[band, :, :, columns].astype(
                jnp.float32
            )
            out_v[band, :, :, columns] = total.astype(jnp.bfloat16)
        for part in range(2):
            out_copy(band, part).start()
        return carry

    lax.fori_loop(0, bands, project, 0)

    def drain(band, carry):
        for part in range(2):
            out_copy(band, part).wait()
        for distance in range(1, members):
            homeward(band, distance).wait_send()
            for kind, part in pieces:
                outgoing(band, distance, kind, part).wait_send()
        return carry

    lax.fori_loop(0, bands, drain, 0)


def fused_device(qkv_grid, tokens, out_weight, regions):
    windows = lax.axis_size("win")
    members = lax.axis_size("seq")
    lat, _, cols, packed = qkv_grid.shape
    bands = lat // WH
    group = D // members
    heads = HEADS // members
    block = WH * cols
    window_tokens = WH * WW
    labels = regions.reshape(lat, WW).astype(jnp.bfloat16)
    behind = from_behind(labels, "win", 1)
    labels = jnp.where(lax.axis_index("seq") < members // 2, behind, labels)
    labels = labels.reshape(bands, WH, members, cols).transpose(0, 2, 1, 3)
    labels = jnp.broadcast_to(
        labels.reshape(bands, window_tokens, 1), (bands, window_tokens, LANES)
    )
    bf16 = jnp.bfloat16
    wide = 2 * LANES
    dma = pltpu.SemaphoreType.DMA
    out = pl.pallas_call(
        functools.partial(fused_kernel, windows, members, bands, cols),
        out_shape=jax.ShapeDtypeStruct((lat, cols, D), bf16),
        in_specs=[pl.BlockSpec(memory_space=pl.ANY)] * 4,
        out_specs=pl.BlockSpec(memory_space=pl.ANY),
        scratch_shapes=[
            pltpu.VMEM((bands, 3, members, WH, cols, group), bf16),
            pltpu.VMEM((bands, window_tokens, LANES), bf16),
            pltpu.VMEM((D, D), bf16),
            pltpu.VMEM((bands, WH, cols, D), bf16),
            pltpu.VMEM((heads, window_tokens, wide), bf16),
            pltpu.VMEM((heads, window_tokens, wide), bf16),
            pltpu.VMEM((heads, window_tokens, wide), bf16),
            pltpu.VMEM((bands, window_tokens, group), bf16),
            pltpu.VMEM((bands, block, D), bf16),
            pltpu.VMEM((bands, WH, cols, D), bf16),
            dma((bands, members - 1, 3, 2)),
            dma((bands, members - 1, 3, 2)),
            dma((bands, 3, 2)),
            dma((bands, members - 1)),
            dma((bands, members - 1)),
            dma((bands,)),
            dma((bands, 2)),
            dma((bands, 2)),
            dma((2,)),
        ],
        compiler_params=pltpu.CompilerParams(
            collective_id=0, has_side_effects=True, vmem_limit_bytes=56 * 1024 * 1024
        ),
    )(
        qkv_grid.reshape(lat, cols, packed),
        tokens.reshape(lat, cols, D),
        out_weight,
        labels,
    )
    return out.reshape(tokens.shape)


def per_device(qkv_grid, tokens, out_weight, regions):
    members = lax.axis_size("seq")
    group = D // members
    fits = members % 2 == 0 and group % LANES == 0 and qkv_grid.shape[2] % ROWS8 == 0
    if fits:
        return fused_device(qkv_grid, tokens, out_weight, regions)
    return general_device(qkv_grid, tokens, out_weight, regions)


def solution(mesh):
    in_specs = (P(None, "win", "seq", None), P(None, "win", "seq", None), P(), P(None, "win", None))
    out_specs = P(None, "win", "seq", None)
    return jax.shard_map(
        per_device, mesh=mesh, in_specs=in_specs, out_specs=out_specs, check_vma=False
    )
```

```python
import functools

import jax
import jax.numpy as jnp
from jax import lax
from jax.experimental import pallas as pl
from jax.experimental.pallas import tpu as pltpu
from jax.sharding import PartitionSpec as P

D = 1536
HEADS = 16
HD = 96
WH = 30
WW = 32


def from_behind(block, axis, distance):
    devices = range(lax.axis_size(axis))
    route = [((i - distance) % len(devices), i) for i in devices]
    return lax.ppermute(block, axis, route)


def attend(window_block, labels):
    queries = window_block[:, 0]
    key_rows = window_block[:, 1]
    values = window_block[:, 2]
    scores = jnp.einsum(
        "qhd,khd->hqk", queries, key_rows, preferred_element_type=jnp.float32
    ) * HD ** (-0.5)
    allowed = labels[:, None] == labels[None, :]
    scores = jnp.where(allowed[None], scores, -1e30)
    largest = jnp.max(scores, axis=-1, keepdims=True)
    weights = jnp.exp(scores - largest)
    soft_weights = (weights / jnp.sum(weights, axis=-1, keepdims=True)).astype(jnp.bfloat16)
    result = jnp.einsum("hqk,khd->qhd", soft_weights, values, preferred_element_type=jnp.float32)
    return result.astype(jnp.bfloat16)


def one_window(paired):
    return attend(paired[0], paired[1])


def window_attention(flat_grid, labels_flat):
    row_total, col_total, three, heads_here, head_size = flat_grid.shape
    bands = row_total // WH
    window_count = col_total // WW
    blocks = flat_grid.reshape(bands, WH, window_count, WW, three, heads_here, head_size)
    blocks = blocks.transpose(0, 2, 1, 3, 4, 5, 6).reshape(
        bands * window_count, WH * WW, three, heads_here, head_size
    )
    labels = (
        labels_flat.reshape(bands, WH, window_count, WW)
        .transpose(0, 2, 1, 3)
        .reshape(bands * window_count, WH * WW)
    )
    attended = lax.map(one_window, (blocks, labels))
    attended = attended.reshape(bands, window_count, WH, WW, heads_here, head_size).transpose(
        0, 2, 1, 3, 4, 5
    )
    return attended.reshape(row_total, col_total, heads_here, head_size)


def general_device(qkv_grid, tokens, out_weight, regions):
    seq_count = lax.axis_size("seq")
    lat_rows, win_count, col_count, packed_width = qkv_grid.shape
    labels_local = regions.reshape(lat_rows, win_count * WW)
    half_cols = WW // 2
    half_rows = WH // 2
    group_heads = HEADS // seq_count
    split_heads = qkv_grid.reshape(lat_rows, win_count, col_count, 3, seq_count, group_heads, HD)
    gathered = lax.all_to_all(split_heads, "seq", split_axis=4, concat_axis=2, tiled=True)
    flat_grid = gathered.reshape(lat_rows, win_count * WW, 3, group_heads, HD)
    arriving = from_behind(flat_grid[:, :half_cols], "win", -1)
    shifted = jnp.concatenate([flat_grid[:, half_cols:], arriving], axis=1)
    shifted = jnp.roll(shifted, -half_rows, axis=0)
    result = window_attention(shifted, labels_local)
    result = jnp.roll(result, half_rows, axis=0)
    leaving = from_behind(result[:, -half_cols:], "win", 1)
    result = jnp.concatenate([leaving, result[:, :-half_cols]], axis=1)
    attended = result.reshape(lat_rows, win_count, WW, 1, group_heads, HD)
    returned = lax.all_to_all(attended, "seq", split_axis=2, concat_axis=3, tiled=True)
    mixed_in = returned.reshape(lat_rows, win_count, col_count, D)
    projected = jnp.dot(mixed_in.reshape(-1, D), out_weight, preferred_element_type=jnp.float32)
    total = projected + tokens.reshape(-1, D).astype(jnp.float32)
    return total.astype(jnp.bfloat16).reshape(tokens.shape)


LANES = 128
ROWS8 = 8
FAR = -1e30
LOG2E = 1.4426950408889634
REGION_SLOTS = 3


def head_span(head):
    first = head * HD // LANES
    last = ((head + 1) * HD - 1) // LANES
    return first, last + 1, head * HD - first * LANES


def spare_lane(head):
    first, last, start = head_span(head)
    return 0 if start > 0 else HD


def fused_kernel(
    windows,
    members,
    bands,
    cols,
    qkv_ref,
    tokens_ref,
    weight_ref,
    label_ref,
    out_ref,
    arrived,
    label_v,
    weight_v,
    token_v,
    q_h,
    k_h,
    v_h,
    result,
    gathered,
    total_v,
    send_sem,
    recv_sem,
    own_sem,
    back_send,
    back_recv,
    back_own,
    token_sem,
    label_sem,
    weight_sem,
):
    half_rows = WH // 2
    half_n = members // 2
    group = D // members
    heads = HEADS // members
    block = WH * cols
    lat = bands * WH
    w = lax.axis_index("win")
    s = lax.axis_index("seq")
    low = 1 - s // half_n
    home = lax.rem(w + windows - low, windows)
    me = lax.rem(s + half_n, members)

    def member_at(distance):
        return lax.rem(me + distance, members)

    def device_of(member):
        seat = lax.rem(member + half_n, members)
        column = lax.rem(home + 1 - seat // half_n, windows)
        return {"win": column, "seq": seat}

    def grid_row(band, part):
        return lax.rem(half_rows * (2 * band + part + 1), lat)

    def features(kind, member):
        return pl.ds(pl.multiple_of(kind * D + member * group, LANES), group)

    def outgoing(band, distance, kind, part):
        target = member_at(distance)
        return pltpu.make_async_remote_copy(
            src_ref=qkv_ref.at[pl.ds(grid_row(band, part), half_rows), :, features(kind, target)],
            dst_ref=arrived.at[band, kind, me, pl.ds(part * half_rows, half_rows)],
            send_sem=send_sem.at[band, distance - 1, kind, part],
            recv_sem=recv_sem.at[band, distance - 1, kind, part],
            device_id=device_of(target),
            device_id_type=pl.DeviceIdType.MESH,
        )

    def own(band, kind, part):
        return pltpu.make_async_copy(
            qkv_ref.at[pl.ds(grid_row(band, part), half_rows), :, features(kind, me)],
            arrived.at[band, kind, me, pl.ds(part * half_rows, half_rows)],
            own_sem.at[band, kind, part],
        )

    def token_copy(band, part):
        return pltpu.make_async_copy(
            tokens_ref.at[pl.ds(grid_row(band, part), half_rows)],
            token_v.at[band, pl.ds(part * half_rows, half_rows)],
            token_sem.at[band, part],
        )

    def rows_of(member):
        return pl.ds(pl.multiple_of(member * block, block), block)

    def homeward(band, distance):
        target = member_at(distance)
        return pltpu.make_async_remote_copy(
            src_ref=result.at[band, rows_of(target)],
            dst_ref=gathered.at[band, :, features(0, me)],
            send_sem=back_send.at[band, distance - 1],
            recv_sem=back_recv.at[band, distance - 1],
            device_id=device_of(target),
            device_id_type=pl.DeviceIdType.MESH,
        )

    def stay(band):
        return pltpu.make_async_copy(
            result.at[band, rows_of(me)],
            gathered.at[band, :, features(0, me)],
            back_own.at[band],
        )

    own_labels = pltpu.make_async_copy(label_ref, label_v, label_sem.at[2])
    sent_labels = pltpu.make_async_remote_copy(
        src_ref=label_ref,
        dst_ref=label_v,
        send_sem=label_sem.at[0],
        recv_sem=label_sem.at[1],
        device_id=device_of(member_at(half_n)),
        device_id_type=pl.DeviceIdType.MESH,
    )
    weight_copy = pltpu.make_async_copy(weight_ref, weight_v, weight_sem)

    barrier = pltpu.get_barrier_semaphore()
    for distance in range(1, members):
        pl.semaphore_signal(
            barrier,
            inc=1,
            device_id=device_of(member_at(distance)),
            device_id_type=pl.DeviceIdType.MESH,
        )
    pl.semaphore_wait(barrier, members - 1)

    pieces = [(kind, part) for kind in range(3) for part in range(2)]

    def launch(band, carry):
        for kind, part in pieces:
            for distance in range(1, members):
                outgoing(band, distance, kind, part).start()
        for kind, part in pieces:
            own(band, kind, part).start()
        return carry

    @pl.when(low == 0)
    def _():
        sent_labels.start()
        own_labels.start()

    lax.fori_loop(0, bands, launch, 0)
    weight_copy.start()
    for band in range(bands):
        for part in range(2):
            token_copy(band, part).start()

    @pl.when(low == 0)
    def _():
        own_labels.wait()

    @pl.when(low == 1)
    def _():
        sent_labels.wait_recv()

    lane = lax.broadcasted_iota(jnp.int32, (block, LANES), 1)
    slot = lax.rem(lane, 32).astype(jnp.float32)
    spread = (WH, cols, WW)
    column_id = lax.broadcasted_iota(jnp.int32, spread, 2)
    cell_id = lax.broadcasted_iota(jnp.int32, spread, 1)

    def prepare(band, member):
        rows = rows_of(member)
        band_labels = label_v[pl.ds(band * WH, WH)].astype(jnp.float32)
        picked = jnp.where(
            column_id == cell_id + member * cols, jnp.broadcast_to(band_labels, spread), 0.0
        )
        label = jnp.broadcast_to(
            jnp.sum(picked, axis=-1, keepdims=True), (WH, cols, LANES)
        ).reshape(block, LANES)
        same = slot == label
        query_fill = jnp.where(same, FAR, 0.0)
        key_fill = jnp.where(same, 0.0, jnp.where(slot < REGION_SLOTS, 1.0, 0.0))
        ones = jnp.ones((block, LANES), jnp.float32)
        for kind, target, fill in ((0, q_h, query_fill), (1, k_h, key_fill), (2, v_h, ones)):
            wide = arrived[band, kind, member].astype(jnp.float32).reshape(block, group)
            for head in range(heads):
                first, last, start = head_span(head)
                for tile in range(first, last):
                    place = lane + (tile - first) * LANES
                    inside = (place >= start) & (place < start + HD)
                    chosen = jnp.where(inside, wide[:, tile * LANES : (tile + 1) * LANES], fill)
                    spot = (tile - first) * LANES
                    target[head, rows, spot : spot + LANES] = chosen.astype(jnp.bfloat16)

    def attend_band(band, carry):
        for kind, part in pieces:
            own(band, kind, part).wait()
            for distance in range(1, members):
                outgoing(band, distance, kind, part).wait_recv()

        def prepare_step(member, inner):
            prepare(band, member)
            return inner

        lax.fori_loop(0, members, prepare_step, 0)

        def query_step(step, inner):
            target = member_at(step + 1)
            rows = rows_of(target)
            tiles = [None] * (group // LANES)
            for head in range(heads):
                first, last, start = head_span(head)
                width = (last - first) * LANES
                scores = lax.dot_general(
                    q_h[head, rows, :width],
                    k_h[head, :, :width],
                    (((1,), (1,)), ((), ())),
                    preferred_element_type=jnp.float32,
                )
                largest = jnp.max(scores, axis=-1, keepdims=True)
                weights = jnp.exp2((scores - largest) * (HD ** (-0.5) * LOG2E))
                mixed = jnp.dot(
                    weights.astype(jnp.bfloat16),
                    v_h[head, :, :width],
                    preferred_element_type=jnp.float32,
                )
                spare = spare_lane(head)
                mixed = mixed * (1.0 / mixed[:, spare : spare + 1])
                for tile in range(first, last):
                    piece = mixed[:, (tile - first) * LANES : (tile - first + 1) * LANES]
                    if tiles[tile] is None:
                        tiles[tile] = piece
                    else:
                        tiles[tile] = jnp.where(lane < head * HD - tile * LANES, tiles[tile], piece)
            for tile, value in enumerate(tiles):
                result[band, rows, tile * LANES : (tile + 1) * LANES] = value.astype(jnp.bfloat16)

            @pl.when(step < members - 1)
            def _():
                homeward(band, step + 1).start()

            @pl.when(step == members - 1)
            def _():
                stay(band).start()

            return inner

        lax.fori_loop(0, members, query_step, 0)
        return carry

    lax.fori_loop(0, bands, attend_band, 0)

    weight_copy.wait()

    def partial_of(band, member, columns):
        return jnp.dot(
            gathered[band, :, features(0, member)],
            weight_v[features(0, member), columns],
            preferred_element_type=jnp.float32,
        )

    def project(band, carry):
        stay(band).wait()
        for part in range(2):
            token_copy(band, part).wait()
        for distance in range(members):
            if distance > 0:
                homeward(band, distance).wait_recv()
            source = member_at(members - distance)
            for start in range(0, D, group):
                columns = slice(start, start + group)
                term = partial_of(band, source, columns)
                if distance == 0:
                    total_v[:, columns] = term
                elif distance < members - 1:
                    total_v[:, columns] += term
                else:
                    total = (total_v[:, columns] + term).reshape(WH, cols, group)
                    total = total + token_v[band, :, :, columns].astype(jnp.float32)
                    total = total.astype(jnp.bfloat16)
                    for part in range(2):
                        out_ref[pl.ds(grid_row(band, part), half_rows), :, columns] = total[
                            part * half_rows : (part + 1) * half_rows
                        ]
        return carry

    lax.fori_loop(0, bands, project, 0)

    @pl.when(low == 0)
    def _():
        sent_labels.wait_send()

    def drain(band, carry):
        for distance in range(1, members):
            homeward(band, distance).wait_send()
            for kind, part in pieces:
                outgoing(band, distance, kind, part).wait_send()
        return carry

    lax.fori_loop(0, bands, drain, 0)


def fused_device(qkv_grid, tokens, out_weight, regions):
    windows = lax.axis_size("win")
    members = lax.axis_size("seq")
    lat, _, cols, packed = qkv_grid.shape
    bands = lat // WH
    group = D // members
    heads = HEADS // members
    block = WH * cols
    window_tokens = WH * WW
    bf16 = jnp.bfloat16
    wide = 2 * LANES
    dma = pltpu.SemaphoreType.DMA
    out = pl.pallas_call(
        functools.partial(fused_kernel, windows, members, bands, cols),
        out_shape=pltpu.VMEM((lat, cols, D), bf16),
        in_specs=[pl.BlockSpec(memory_space=pl.ANY)] * 4,
        out_specs=pl.BlockSpec(memory_space=pltpu.VMEM),
        scratch_shapes=[
            pltpu.VMEM((bands, 3, members, WH, cols, group), bf16),
            pltpu.VMEM((lat, 1, WW), jnp.int32),
            pltpu.VMEM((D, D), bf16),
            pltpu.VMEM((bands, WH, cols, D), bf16),
            pltpu.VMEM((heads, window_tokens, wide), bf16),
            pltpu.VMEM((heads, window_tokens, wide), bf16),
            pltpu.VMEM((heads, window_tokens, wide), bf16),
            pltpu.VMEM((bands, window_tokens, group), bf16),
            pltpu.VMEM((bands, block, D), bf16),
            pltpu.VMEM((block, D), jnp.float32),
            dma((bands, members - 1, 3, 2)),
            dma((bands, members - 1, 3, 2)),
            dma((bands, 3, 2)),
            dma((bands, members - 1)),
            dma((bands, members - 1)),
            dma((bands,)),
            dma((bands, 2)),
            dma((3,)),
            dma,
        ],
        compiler_params=pltpu.CompilerParams(
            collective_id=0, has_side_effects=True, vmem_limit_bytes=56 * 1024 * 1024
        ),
    )(
        qkv_grid.reshape(lat, cols, packed),
        tokens.reshape(lat, cols, D),
        out_weight,
        regions,
    )
    return out.reshape(tokens.shape)


def per_device(qkv_grid, tokens, out_weight, regions):
    members = lax.axis_size("seq")
    group = D // members
    fits = members % 2 == 0 and group % LANES == 0 and qkv_grid.shape[2] % ROWS8 == 0
    if fits:
        return fused_device(qkv_grid, tokens, out_weight, regions)
    return general_device(qkv_grid, tokens, out_weight, regions)


def solution(mesh):
    in_specs = (P(None, "win", "seq", None), P(None, "win", "seq", None), P(), P(None, "win", None))
    out_specs = P(None, "win", "seq", None)
    return jax.shard_map(
        per_device, mesh=mesh, in_specs=in_specs, out_specs=out_specs, check_vma=False
    )
```

```python
import functools

import jax
import jax.numpy as jnp
from jax import lax
from jax.experimental import pallas as pl
from jax.experimental.pallas import tpu as pltpu
from jax.sharding import PartitionSpec as P

D = 1536
HEADS = 16
HD = 96
WH = 30
WW = 32


def from_behind(block, axis, distance):
    devices = range(lax.axis_size(axis))
    route = [((i - distance) % len(devices), i) for i in devices]
    return lax.ppermute(block, axis, route)


def attend(window_block, labels):
    queries = window_block[:, 0]
    key_rows = window_block[:, 1]
    values = window_block[:, 2]
    scores = jnp.einsum(
        "qhd,khd->hqk", queries, key_rows, preferred_element_type=jnp.float32
    ) * HD ** (-0.5)
    allowed = labels[:, None] == labels[None, :]
    scores = jnp.where(allowed[None], scores, -1e30)
    largest = jnp.max(scores, axis=-1, keepdims=True)
    weights = jnp.exp(scores - largest)
    soft_weights = (weights / jnp.sum(weights, axis=-1, keepdims=True)).astype(jnp.bfloat16)
    result = jnp.einsum("hqk,khd->qhd", soft_weights, values, preferred_element_type=jnp.float32)
    return result.astype(jnp.bfloat16)


def one_window(paired):
    return attend(paired[0], paired[1])


def window_attention(flat_grid, labels_flat):
    row_total, col_total, three, heads_here, head_size = flat_grid.shape
    bands = row_total // WH
    window_count = col_total // WW
    blocks = flat_grid.reshape(bands, WH, window_count, WW, three, heads_here, head_size)
    blocks = blocks.transpose(0, 2, 1, 3, 4, 5, 6).reshape(
        bands * window_count, WH * WW, three, heads_here, head_size
    )
    labels = (
        labels_flat.reshape(bands, WH, window_count, WW)
        .transpose(0, 2, 1, 3)
        .reshape(bands * window_count, WH * WW)
    )
    attended = lax.map(one_window, (blocks, labels))
    attended = attended.reshape(bands, window_count, WH, WW, heads_here, head_size).transpose(
        0, 2, 1, 3, 4, 5
    )
    return attended.reshape(row_total, col_total, heads_here, head_size)


def general_device(qkv_grid, tokens, out_weight, regions):
    seq_count = lax.axis_size("seq")
    lat_rows, win_count, col_count, packed_width = qkv_grid.shape
    labels_local = regions.reshape(lat_rows, win_count * WW)
    half_cols = WW // 2
    half_rows = WH // 2
    group_heads = HEADS // seq_count
    split_heads = qkv_grid.reshape(lat_rows, win_count, col_count, 3, seq_count, group_heads, HD)
    gathered = lax.all_to_all(split_heads, "seq", split_axis=4, concat_axis=2, tiled=True)
    flat_grid = gathered.reshape(lat_rows, win_count * WW, 3, group_heads, HD)
    arriving = from_behind(flat_grid[:, :half_cols], "win", -1)
    shifted = jnp.concatenate([flat_grid[:, half_cols:], arriving], axis=1)
    shifted = jnp.roll(shifted, -half_rows, axis=0)
    result = window_attention(shifted, labels_local)
    result = jnp.roll(result, half_rows, axis=0)
    leaving = from_behind(result[:, -half_cols:], "win", 1)
    result = jnp.concatenate([leaving, result[:, :-half_cols]], axis=1)
    attended = result.reshape(lat_rows, win_count, WW, 1, group_heads, HD)
    returned = lax.all_to_all(attended, "seq", split_axis=2, concat_axis=3, tiled=True)
    mixed_in = returned.reshape(lat_rows, win_count, col_count, D)
    projected = jnp.dot(mixed_in.reshape(-1, D), out_weight, preferred_element_type=jnp.float32)
    total = projected + tokens.reshape(-1, D).astype(jnp.float32)
    return total.astype(jnp.bfloat16).reshape(tokens.shape)


LANES = 128
ROWS8 = 8
FAR = -1e30
LOG2E = 1.4426950408889634
REGION_SLOTS = 3


def head_span(head):
    first = head * HD // LANES
    last = ((head + 1) * HD - 1) // LANES
    return first, last + 1, head * HD - first * LANES


def spare_lane(head):
    first, last, start = head_span(head)
    return 0 if start > 0 else HD


def fused_kernel(
    windows,
    members,
    bands,
    cols,
    qkv_ref,
    tokens_ref,
    weight_ref,
    label_ref,
    out_ref,
    arrived,
    label_v,
    weight_v,
    token_v,
    q_h,
    k_h,
    v_h,
    result,
    gathered,
    total_v,
    send_sem,
    recv_sem,
    own_sem,
    back_send,
    back_recv,
    back_own,
    token_sem,
    label_sem,
    weight_sem,
):
    half_rows = WH // 2
    half_n = members // 2
    group = D // members
    heads = HEADS // members
    block = WH * cols
    lat = bands * WH
    w = lax.axis_index("win")
    s = lax.axis_index("seq")
    low = 1 - s // half_n
    home = lax.rem(w + windows - low, windows)
    me = lax.rem(s + half_n, members)

    def member_at(distance):
        return lax.rem(me + distance, members)

    def device_of(member):
        seat = lax.rem(member + half_n, members)
        column = lax.rem(home + 1 - seat // half_n, windows)
        return {"win": column, "seq": seat}

    def grid_row(band, part):
        return lax.rem(half_rows * (2 * band + part + 1), lat)

    def features(kind, member):
        return pl.ds(pl.multiple_of(kind * D + member * group, LANES), group)

    def outgoing(band, distance, kind, part):
        target = member_at(distance)
        return pltpu.make_async_remote_copy(
            src_ref=qkv_ref.at[pl.ds(grid_row(band, part), half_rows), :, features(kind, target)],
            dst_ref=arrived.at[band, kind, me, pl.ds(part * half_rows, half_rows)],
            send_sem=send_sem.at[band, distance - 1, kind, part],
            recv_sem=recv_sem.at[band, distance - 1, kind, part],
            device_id=device_of(target),
            device_id_type=pl.DeviceIdType.MESH,
        )

    def own(band, kind, part):
        return pltpu.make_async_copy(
            qkv_ref.at[pl.ds(grid_row(band, part), half_rows), :, features(kind, me)],
            arrived.at[band, kind, me, pl.ds(part * half_rows, half_rows)],
            own_sem.at[band, kind, part],
        )

    def token_copy(band, part):
        return pltpu.make_async_copy(
            tokens_ref.at[pl.ds(grid_row(band, part), half_rows)],
            token_v.at[band, pl.ds(part * half_rows, half_rows)],
            token_sem.at[band, part],
        )

    def rows_of(member):
        return pl.ds(pl.multiple_of(member * block, block), block)

    def homeward(band, distance):
        target = member_at(distance)
        return pltpu.make_async_remote_copy(
            src_ref=result.at[band, rows_of(target)],
            dst_ref=gathered.at[band, :, features(0, me)],
            send_sem=back_send.at[band, distance - 1],
            recv_sem=back_recv.at[band, distance - 1],
            device_id=device_of(target),
            device_id_type=pl.DeviceIdType.MESH,
        )

    def stay(band):
        return pltpu.make_async_copy(
            result.at[band, rows_of(me)],
            gathered.at[band, :, features(0, me)],
            back_own.at[band],
        )

    own_labels = pltpu.make_async_copy(label_ref, label_v, label_sem.at[2])
    sent_labels = pltpu.make_async_remote_copy(
        src_ref=label_ref,
        dst_ref=label_v,
        send_sem=label_sem.at[0],
        recv_sem=label_sem.at[1],
        device_id=device_of(member_at(half_n)),
        device_id_type=pl.DeviceIdType.MESH,
    )
    weight_copy = pltpu.make_async_copy(weight_ref, weight_v, weight_sem)

    barrier = pltpu.get_barrier_semaphore()
    for distance in range(1, members):
        pl.semaphore_signal(
            barrier,
            inc=1,
            device_id=device_of(member_at(distance)),
            device_id_type=pl.DeviceIdType.MESH,
        )
    pl.semaphore_wait(barrier, members - 1)

    pieces = [(kind, part) for kind in range(3) for part in range(2)]

    def launch(band, carry):
        for kind, part in pieces:
            for distance in range(1, members):
                outgoing(band, distance, kind, part).start()
        for kind, part in pieces:
            own(band, kind, part).start()
        return carry

    @pl.when(low == 0)
    def _():
        sent_labels.start()
        own_labels.start()

    lax.fori_loop(0, bands, launch, 0)
    weight_copy.start()
    for band in range(bands):
        for part in range(2):
            token_copy(band, part).start()

    @pl.when(low == 0)
    def _():
        own_labels.wait()

    @pl.when(low == 1)
    def _():
        sent_labels.wait_recv()

    lane = lax.broadcasted_iota(jnp.int32, (block, LANES), 1)
    slot = lax.rem(lane, 32).astype(jnp.float32)
    spread = (WH, cols, lat)
    row_lane = lax.broadcasted_iota(jnp.int32, spread, 2)
    row_id = lax.broadcasted_iota(jnp.int32, spread, 0)

    def prepare(band, member):
        rows = rows_of(member)
        seats = pl.ds(pl.multiple_of(member * cols, cols), cols)
        member_labels = label_v[:, seats, :].astype(jnp.float32)
        picked = jnp.where(
            row_lane == row_id + band * WH, jnp.broadcast_to(member_labels, spread), 0.0
        )
        label = jnp.broadcast_to(
            jnp.sum(picked, axis=-1, keepdims=True), (WH, cols, LANES)
        ).reshape(block, LANES)
        same = slot == label
        query_fill = jnp.where(same, FAR, 0.0)
        key_fill = jnp.where(same, 0.0, jnp.where(slot < REGION_SLOTS, 1.0, 0.0))
        ones = jnp.ones((block, LANES), jnp.float32)
        for kind, target, fill in ((0, q_h, query_fill), (1, k_h, key_fill), (2, v_h, ones)):
            wide = arrived[band, kind, member].astype(jnp.float32).reshape(block, group)
            for head in range(heads):
                first, last, start = head_span(head)
                for tile in range(first, last):
                    place = lane + (tile - first) * LANES
                    inside = (place >= start) & (place < start + HD)
                    chosen = jnp.where(inside, wide[:, tile * LANES : (tile + 1) * LANES], fill)
                    spot = (tile - first) * LANES
                    target[head, rows, spot : spot + LANES] = chosen.astype(jnp.bfloat16)

    def attend_band(band, carry):
        for kind, part in pieces:
            own(band, kind, part).wait()
            for distance in range(1, members):
                outgoing(band, distance, kind, part).wait_recv()

        def prepare_step(member, inner):
            prepare(band, member)
            return inner

        lax.fori_loop(0, members, prepare_step, 0)

        def query_step(step, inner):
            target = member_at(step + 1)
            rows = rows_of(target)
            tiles = [None] * (group // LANES)
            for head in range(heads):
                first, last, start = head_span(head)
                width = (last - first) * LANES
                scores = lax.dot_general(
                    q_h[head, rows, :width],
                    k_h[head, :, :width],
                    (((1,), (1,)), ((), ())),
                    preferred_element_type=jnp.float32,
                )
                largest = jnp.max(scores, axis=-1, keepdims=True)
                weights = jnp.exp2((scores - largest) * (HD ** (-0.5) * LOG2E))
                mixed = jnp.dot(
                    weights.astype(jnp.bfloat16),
                    v_h[head, :, :width],
                    preferred_element_type=jnp.float32,
                )
                spare = spare_lane(head)
                mixed = mixed * (1.0 / mixed[:, spare : spare + 1])
                for tile in range(first, last):
                    piece = mixed[:, (tile - first) * LANES : (tile - first + 1) * LANES]
                    if tiles[tile] is None:
                        tiles[tile] = piece
                    else:
                        tiles[tile] = jnp.where(lane < head * HD - tile * LANES, tiles[tile], piece)
            for tile, value in enumerate(tiles):
                result[band, rows, tile * LANES : (tile + 1) * LANES] = value.astype(jnp.bfloat16)

            @pl.when(step < members - 1)
            def _():
                homeward(band, step + 1).start()

            @pl.when(step == members - 1)
            def _():
                stay(band).start()

            return inner

        lax.fori_loop(0, members, query_step, 0)
        return carry

    lax.fori_loop(0, bands, attend_band, 0)

    weight_copy.wait()

    def partial_of(band, member, columns):
        return jnp.dot(
            gathered[band, :, features(0, member)],
            weight_v[features(0, member), columns],
            preferred_element_type=jnp.float32,
        )

    def project(band, carry):
        stay(band).wait()
        for part in range(2):
            token_copy(band, part).wait()
        for distance in range(members):
            if distance > 0:
                homeward(band, distance).wait_recv()
            source = member_at(members - distance)
            for start in range(0, D, group):
                columns = slice(start, start + group)
                term = partial_of(band, source, columns)
                if distance == 0:
                    total_v[:, columns] = term
                elif distance < members - 1:
                    total_v[:, columns] += term
                else:
                    total = (total_v[:, columns] + term).reshape(WH, cols, group)
                    total = total + token_v[band, :, :, columns].astype(jnp.float32)
                    total = total.astype(jnp.bfloat16)
                    for part in range(2):
                        out_ref[pl.ds(grid_row(band, part), half_rows), :, columns] = total[
                            part * half_rows : (part + 1) * half_rows
                        ]
        return carry

    lax.fori_loop(0, bands, project, 0)

    @pl.when(low == 0)
    def _():
        sent_labels.wait_send()

    def drain(band, carry):
        for distance in range(1, members):
            homeward(band, distance).wait_send()
            for kind, part in pieces:
                outgoing(band, distance, kind, part).wait_send()
        return carry

    lax.fori_loop(0, bands, drain, 0)


def fused_device(qkv_grid, tokens, out_weight, regions):
    windows = lax.axis_size("win")
    members = lax.axis_size("seq")
    lat, _, cols, packed = qkv_grid.shape
    bands = lat // WH
    group = D // members
    heads = HEADS // members
    block = WH * cols
    window_tokens = WH * WW
    bf16 = jnp.bfloat16
    wide = 2 * LANES
    dma = pltpu.SemaphoreType.DMA
    out = pl.pallas_call(
        functools.partial(fused_kernel, windows, members, bands, cols),
        out_shape=pltpu.VMEM((lat, cols, D), bf16),
        in_specs=[pl.BlockSpec(memory_space=pl.ANY)] * 4,
        out_specs=pl.BlockSpec(memory_space=pltpu.VMEM),
        scratch_shapes=[
            pltpu.VMEM((bands, 3, members, WH, cols, group), bf16),
            pltpu.VMEM((1, WW, lat), jnp.int32),
            pltpu.VMEM((D, D), bf16),
            pltpu.VMEM((bands, WH, cols, D), bf16),
            pltpu.VMEM((heads, window_tokens, wide), bf16),
            pltpu.VMEM((heads, window_tokens, wide), bf16),
            pltpu.VMEM((heads, window_tokens, wide), bf16),
            pltpu.VMEM((bands, window_tokens, group), bf16),
            pltpu.VMEM((bands, block, D), bf16),
            pltpu.VMEM((block, D), jnp.float32),
            dma((bands, members - 1, 3, 2)),
            dma((bands, members - 1, 3, 2)),
            dma((bands, 3, 2)),
            dma((bands, members - 1)),
            dma((bands, members - 1)),
            dma((bands,)),
            dma((bands, 2)),
            dma((3,)),
            dma,
        ],
        compiler_params=pltpu.CompilerParams(
            collective_id=0, has_side_effects=True, vmem_limit_bytes=56 * 1024 * 1024
        ),
    )(
        qkv_grid.reshape(lat, cols, packed),
        tokens.reshape(lat, cols, D),
        out_weight,
        regions.transpose(1, 2, 0),
    )
    return out.reshape(tokens.shape)


def per_device(qkv_grid, tokens, out_weight, regions):
    members = lax.axis_size("seq")
    group = D // members
    fits = members % 2 == 0 and group % LANES == 0 and qkv_grid.shape[2] % ROWS8 == 0
    if fits:
        return fused_device(qkv_grid, tokens, out_weight, regions)
    return general_device(qkv_grid, tokens, out_weight, regions)


def solution(mesh):
    in_specs = (P(None, "win", "seq", None), P(None, "win", "seq", None), P(), P(None, "win", None))
    out_specs = P(None, "win", "seq", None)
    return jax.shard_map(
        per_device, mesh=mesh, in_specs=in_specs, out_specs=out_specs, check_vma=False
    )
```

```python
import functools

import jax
import jax.numpy as jnp
from jax import lax
from jax.experimental import pallas as pl
from jax.experimental.pallas import tpu as pltpu
from jax.sharding import PartitionSpec as P

D = 1536
HEADS = 16
HD = 96
WH = 30
WW = 32


def from_behind(block, axis, distance):
    devices = range(lax.axis_size(axis))
    route = [((i - distance) % len(devices), i) for i in devices]
    return lax.ppermute(block, axis, route)


def attend(window_block, labels):
    queries = window_block[:, 0]
    key_rows = window_block[:, 1]
    values = window_block[:, 2]
    scores = jnp.einsum(
        "qhd,khd->hqk", queries, key_rows, preferred_element_type=jnp.float32
    ) * HD ** (-0.5)
    allowed = labels[:, None] == labels[None, :]
    scores = jnp.where(allowed[None], scores, -1e30)
    largest = jnp.max(scores, axis=-1, keepdims=True)
    weights = jnp.exp(scores - largest)
    soft_weights = (weights / jnp.sum(weights, axis=-1, keepdims=True)).astype(jnp.bfloat16)
    result = jnp.einsum("hqk,khd->qhd", soft_weights, values, preferred_element_type=jnp.float32)
    return result.astype(jnp.bfloat16)


def one_window(paired):
    return attend(paired[0], paired[1])


def window_attention(flat_grid, labels_flat):
    row_total, col_total, three, heads_here, head_size = flat_grid.shape
    bands = row_total // WH
    window_count = col_total // WW
    blocks = flat_grid.reshape(bands, WH, window_count, WW, three, heads_here, head_size)
    blocks = blocks.transpose(0, 2, 1, 3, 4, 5, 6).reshape(
        bands * window_count, WH * WW, three, heads_here, head_size
    )
    labels = (
        labels_flat.reshape(bands, WH, window_count, WW)
        .transpose(0, 2, 1, 3)
        .reshape(bands * window_count, WH * WW)
    )
    attended = lax.map(one_window, (blocks, labels))
    attended = attended.reshape(bands, window_count, WH, WW, heads_here, head_size).transpose(
        0, 2, 1, 3, 4, 5
    )
    return attended.reshape(row_total, col_total, heads_here, head_size)


def general_device(qkv_grid, tokens, out_weight, regions):
    seq_count = lax.axis_size("seq")
    lat_rows, win_count, col_count, packed_width = qkv_grid.shape
    labels_local = regions.reshape(lat_rows, win_count * WW)
    half_cols = WW // 2
    half_rows = WH // 2
    group_heads = HEADS // seq_count
    split_heads = qkv_grid.reshape(lat_rows, win_count, col_count, 3, seq_count, group_heads, HD)
    gathered = lax.all_to_all(split_heads, "seq", split_axis=4, concat_axis=2, tiled=True)
    flat_grid = gathered.reshape(lat_rows, win_count * WW, 3, group_heads, HD)
    arriving = from_behind(flat_grid[:, :half_cols], "win", -1)
    shifted = jnp.concatenate([flat_grid[:, half_cols:], arriving], axis=1)
    shifted = jnp.roll(shifted, -half_rows, axis=0)
    result = window_attention(shifted, labels_local)
    result = jnp.roll(result, half_rows, axis=0)
    leaving = from_behind(result[:, -half_cols:], "win", 1)
    result = jnp.concatenate([leaving, result[:, :-half_cols]], axis=1)
    attended = result.reshape(lat_rows, win_count, WW, 1, group_heads, HD)
    returned = lax.all_to_all(attended, "seq", split_axis=2, concat_axis=3, tiled=True)
    mixed_in = returned.reshape(lat_rows, win_count, col_count, D)
    projected = jnp.dot(mixed_in.reshape(-1, D), out_weight, preferred_element_type=jnp.float32)
    total = projected + tokens.reshape(-1, D).astype(jnp.float32)
    return total.astype(jnp.bfloat16).reshape(tokens.shape)


LANES = 128
ROWS8 = 8
FAR = -1e30
LOG2E = 1.4426950408889634
REGION_SLOTS = 3


def head_span(head):
    first = head * HD // LANES
    last = ((head + 1) * HD - 1) // LANES
    return first, last + 1, head * HD - first * LANES


def spare_lane(head):
    first, last, start = head_span(head)
    return 0 if start > 0 else HD


def fused_kernel(
    windows,
    members,
    bands,
    cols,
    qkv_ref,
    tokens_ref,
    weight_ref,
    label_ref,
    out_ref,
    arrived,
    label_v,
    weight_v,
    token_v,
    q_h,
    k_h,
    v_h,
    result,
    gathered,
    total_v,
    send_sem,
    recv_sem,
    own_sem,
    back_send,
    back_recv,
    back_own,
    token_sem,
    label_sem,
    weight_sem,
):
    half_rows = WH // 2
    half_n = members // 2
    group = D // members
    heads = HEADS // members
    block = WH * cols
    lat = bands * WH
    w = lax.axis_index("win")
    s = lax.axis_index("seq")
    low = 1 - s // half_n
    home = lax.rem(w + windows - low, windows)
    me = lax.rem(s + half_n, members)

    def member_at(distance):
        return lax.rem(me + distance, members)

    def device_of(member):
        seat = lax.rem(member + half_n, members)
        column = lax.rem(home + 1 - seat // half_n, windows)
        return {"win": column, "seq": seat}

    def grid_row(band, part):
        return lax.rem(half_rows * (2 * band + part + 1), lat)

    def features(kind, member):
        return pl.ds(pl.multiple_of(kind * D + member * group, LANES), group)

    def outgoing(band, distance, kind, part):
        target = member_at(distance)
        return pltpu.make_async_remote_copy(
            src_ref=qkv_ref.at[pl.ds(grid_row(band, part), half_rows), :, features(kind, target)],
            dst_ref=arrived.at[band, kind, me, pl.ds(part * half_rows, half_rows)],
            send_sem=send_sem.at[band, distance - 1, kind, part],
            recv_sem=recv_sem.at[band, distance - 1, kind, part],
            device_id=device_of(target),
            device_id_type=pl.DeviceIdType.MESH,
        )

    def own(band, kind, part):
        return pltpu.make_async_copy(
            qkv_ref.at[pl.ds(grid_row(band, part), half_rows), :, features(kind, me)],
            arrived.at[band, kind, me, pl.ds(part * half_rows, half_rows)],
            own_sem.at[band, kind, part],
        )

    def token_copy(band, part):
        return pltpu.make_async_copy(
            tokens_ref.at[pl.ds(grid_row(band, part), half_rows)],
            token_v.at[band, pl.ds(part * half_rows, half_rows)],
            token_sem.at[band, part],
        )

    def rows_of(member):
        return pl.ds(pl.multiple_of(member * block, block), block)

    def homeward(band, distance):
        target = member_at(distance)
        return pltpu.make_async_remote_copy(
            src_ref=result.at[band, rows_of(target)],
            dst_ref=gathered.at[band, :, features(0, me)],
            send_sem=back_send.at[band, distance - 1],
            recv_sem=back_recv.at[band, distance - 1],
            device_id=device_of(target),
            device_id_type=pl.DeviceIdType.MESH,
        )

    def stay(band):
        return pltpu.make_async_copy(
            result.at[band, rows_of(me)],
            gathered.at[band, :, features(0, me)],
            back_own.at[band],
        )

    own_labels = pltpu.make_async_copy(label_ref, label_v, label_sem.at[2])
    sent_labels = pltpu.make_async_remote_copy(
        src_ref=label_ref,
        dst_ref=label_v,
        send_sem=label_sem.at[0],
        recv_sem=label_sem.at[1],
        device_id=device_of(member_at(half_n)),
        device_id_type=pl.DeviceIdType.MESH,
    )
    weight_copy = pltpu.make_async_copy(weight_ref, weight_v, weight_sem)

    barrier = pltpu.get_barrier_semaphore()
    for distance in range(1, members):
        pl.semaphore_signal(
            barrier,
            inc=1,
            device_id=device_of(member_at(distance)),
            device_id_type=pl.DeviceIdType.MESH,
        )
    pl.semaphore_wait(barrier, members - 1)

    pieces = [(kind, part) for kind in range(3) for part in range(2)]

    def launch(band, carry):
        for distance in [*range(members // 2, members), *range(1, members // 2)]:
            for kind, part in pieces:
                outgoing(band, distance, kind, part).start()
        for kind, part in pieces:
            own(band, kind, part).start()
        return carry

    @pl.when(low == 0)
    def _():
        sent_labels.start()
        own_labels.start()

    lax.fori_loop(0, bands, launch, 0)
    weight_copy.start()
    for band in range(bands):
        for part in range(2):
            token_copy(band, part).start()

    @pl.when(low == 0)
    def _():
        own_labels.wait()

    @pl.when(low == 1)
    def _():
        sent_labels.wait_recv()

    lane = lax.broadcasted_iota(jnp.int32, (block, LANES), 1)
    slot = lax.rem(lane, 32).astype(jnp.float32)
    spread = (WH, cols, lat)
    row_lane = lax.broadcasted_iota(jnp.int32, spread, 2)
    row_id = lax.broadcasted_iota(jnp.int32, spread, 0)

    def prepare(band, member):
        rows = rows_of(member)
        seats = pl.ds(pl.multiple_of(member * cols, cols), cols)
        member_labels = label_v[:, seats, :].astype(jnp.float32)
        picked = jnp.where(
            row_lane == row_id + band * WH, jnp.broadcast_to(member_labels, spread), 0.0
        )
        label = jnp.broadcast_to(
            jnp.sum(picked, axis=-1, keepdims=True), (WH, cols, LANES)
        ).reshape(block, LANES)
        same = slot == label
        query_fill = jnp.where(same, FAR, 0.0)
        key_fill = jnp.where(same, 0.0, jnp.where(slot < REGION_SLOTS, 1.0, 0.0))
        ones = jnp.ones((block, LANES), jnp.float32)
        for kind, target, fill in ((0, q_h, query_fill), (1, k_h, key_fill), (2, v_h, ones)):
            wide = arrived[band, kind, member].astype(jnp.float32).reshape(block, group)
            for head in range(heads):
                first, last, start = head_span(head)
                for tile in range(first, last):
                    place = lane + (tile - first) * LANES
                    inside = (place >= start) & (place < start + HD)
                    chosen = jnp.where(inside, wide[:, tile * LANES : (tile + 1) * LANES], fill)
                    spot = (tile - first) * LANES
                    target[head, rows, spot : spot + LANES] = chosen.astype(jnp.bfloat16)

    def attend_band(band, carry):
        for kind, part in pieces:
            own(band, kind, part).wait()
            for distance in range(1, members):
                outgoing(band, distance, kind, part).wait_recv()

        def prepare_step(member, inner):
            prepare(band, member)
            return inner

        lax.fori_loop(0, members, prepare_step, 0)

        def query_step(step, inner):
            target = member_at(step + 1)
            rows = rows_of(target)
            tiles = [None] * (group // LANES)
            for head in range(heads):
                first, last, start = head_span(head)
                width = (last - first) * LANES
                scores = lax.dot_general(
                    q_h[head, rows, :width],
                    k_h[head, :, :width],
                    (((1,), (1,)), ((), ())),
                    preferred_element_type=jnp.float32,
                )
                largest = jnp.max(scores, axis=-1, keepdims=True)
                weights = jnp.exp2((scores - largest) * (HD ** (-0.5) * LOG2E))
                mixed = jnp.dot(
                    weights.astype(jnp.bfloat16),
                    v_h[head, :, :width],
                    preferred_element_type=jnp.float32,
                )
                spare = spare_lane(head)
                mixed = mixed * (1.0 / mixed[:, spare : spare + 1])
                for tile in range(first, last):
                    piece = mixed[:, (tile - first) * LANES : (tile - first + 1) * LANES]
                    if tiles[tile] is None:
                        tiles[tile] = piece
                    else:
                        tiles[tile] = jnp.where(lane < head * HD - tile * LANES, tiles[tile], piece)
            for tile, value in enumerate(tiles):
                result[band, rows, tile * LANES : (tile + 1) * LANES] = value.astype(jnp.bfloat16)

            @pl.when(step < members - 1)
            def _():
                homeward(band, step + 1).start()

            @pl.when(step == members - 1)
            def _():
                stay(band).start()

            return inner

        lax.fori_loop(0, members, query_step, 0)
        return carry

    lax.fori_loop(0, bands, attend_band, 0)

    weight_copy.wait()

    def partial_of(band, member, columns):
        return jnp.dot(
            gathered[band, :, features(0, member)],
            weight_v[features(0, member), columns],
            preferred_element_type=jnp.float32,
        )

    def project(band, carry):
        stay(band).wait()
        for part in range(2):
            token_copy(band, part).wait()
        for distance in range(members):
            if distance > 0:
                homeward(band, distance).wait_recv()
            source = member_at(members - distance)
            for start in range(0, D, group):
                columns = slice(start, start + group)
                term = partial_of(band, source, columns)
                if distance == 0:
                    total_v[:, columns] = term
                elif distance < members - 1:
                    total_v[:, columns] += term
                else:
                    total = (total_v[:, columns] + term).reshape(WH, cols, group)
                    total = total + token_v[band, :, :, columns].astype(jnp.float32)
                    total = total.astype(jnp.bfloat16)
                    for part in range(2):
                        out_ref[pl.ds(grid_row(band, part), half_rows), :, columns] = total[
                            part * half_rows : (part + 1) * half_rows
                        ]
        return carry

    lax.fori_loop(0, bands, project, 0)

    @pl.when(low == 0)
    def _():
        sent_labels.wait_send()

    def drain(band, carry):
        for distance in range(1, members):
            homeward(band, distance).wait_send()
            for kind, part in pieces:
                outgoing(band, distance, kind, part).wait_send()
        return carry

    lax.fori_loop(0, bands, drain, 0)


def fused_device(qkv_grid, tokens, out_weight, regions):
    windows = lax.axis_size("win")
    members = lax.axis_size("seq")
    lat, _, cols, packed = qkv_grid.shape
    bands = lat // WH
    group = D // members
    heads = HEADS // members
    block = WH * cols
    window_tokens = WH * WW
    bf16 = jnp.bfloat16
    wide = 2 * LANES
    dma = pltpu.SemaphoreType.DMA
    out = pl.pallas_call(
        functools.partial(fused_kernel, windows, members, bands, cols),
        out_shape=pltpu.VMEM((lat, cols, D), bf16),
        in_specs=[pl.BlockSpec(memory_space=pl.ANY)] * 4,
        out_specs=pl.BlockSpec(memory_space=pltpu.VMEM),
        scratch_shapes=[
            pltpu.VMEM((bands, 3, members, WH, cols, group), bf16),
            pltpu.VMEM((1, WW, lat), jnp.int32),
            pltpu.VMEM((D, D), bf16),
            pltpu.VMEM((bands, WH, cols, D), bf16),
            pltpu.VMEM((heads, window_tokens, wide), bf16),
            pltpu.VMEM((heads, window_tokens, wide), bf16),
            pltpu.VMEM((heads, window_tokens, wide), bf16),
            pltpu.VMEM((bands, window_tokens, group), bf16),
            pltpu.VMEM((bands, block, D), bf16),
            pltpu.VMEM((block, D), jnp.float32),
            dma((bands, members - 1, 3, 2)),
            dma((bands, members - 1, 3, 2)),
            dma((bands, 3, 2)),
            dma((bands, members - 1)),
            dma((bands, members - 1)),
            dma((bands,)),
            dma((bands, 2)),
            dma((3,)),
            dma,
        ],
        compiler_params=pltpu.CompilerParams(
            collective_id=0, has_side_effects=True, vmem_limit_bytes=56 * 1024 * 1024
        ),
    )(
        qkv_grid.reshape(lat, cols, packed),
        tokens.reshape(lat, cols, D),
        out_weight,
        regions.transpose(1, 2, 0),
    )
    return out.reshape(tokens.shape)


def per_device(qkv_grid, tokens, out_weight, regions):
    members = lax.axis_size("seq")
    group = D // members
    fits = members % 2 == 0 and group % LANES == 0 and qkv_grid.shape[2] % ROWS8 == 0
    if fits:
        return fused_device(qkv_grid, tokens, out_weight, regions)
    return general_device(qkv_grid, tokens, out_weight, regions)


def solution(mesh):
    in_specs = (P(None, "win", "seq", None), P(None, "win", "seq", None), P(), P(None, "win", None))
    out_specs = P(None, "win", "seq", None)
    return jax.shard_map(
        per_device, mesh=mesh, in_specs=in_specs, out_specs=out_specs, check_vma=False
    )
```
